32 devices in a mesh: seq: 8 (over z, y), head: 4 (over x, core).
Axes of the slice: x: 2, y: 2, z: 4, core: 2. Of those that a mesh axis runs over, the one named last changes fastest.
Arguments:
- tokens: bfloat16 [16384, 1024], P(('seq', 'head')), may hold values from -6 to 6
- mod_shift: float32 [1024], replicated, may hold values from -3 to 3
- mod_scale: float32 [1024], replicated, may hold values from -3 to 3
- attn_gate: float32 [1024], replicated, may hold values from -4 to 4
- w_qkv: bfloat16 [1024, 3072], replicated, may hold values from -0.1875 to 0.1875
- query_gain: float32 [1024], replicated, may hold values from 0.5 to 8
- key_gain: float32 [1024], replicated, may hold values from 0.5 to 8
- w_out: bfloat16 [1024, 1024], replicated, may hold values from -0.1875 to 0.1875
- w_dec: bfloat16 [1024, 128], replicated, may hold values from -0.1875 to 0.1875
- conv_weight: bfloat16 [3456, 128], replicated, may hold values from -0.109375 to 0.109375
- block_lists: int32 [256, 8], P('seq'), may hold values from 0 to 255, as said below
- active_blocks: int32 [32], replicated, may hold values from 4 to 8
- to_next: int32 [4096], P(('seq', 'head')), may hold values from 0 to 511
- to_prev: int32 [4096], P(('seq', 'head')), may hold values from 0 to 511
- conv_table: int32 [16384, 27], P(('seq', 'head')), may hold values from 0 to 768
Outputs:
- block_out: bfloat16 [16384, 1024], P(('seq', 'head'))
- decoded: bfloat16 [16384, 128], P(('seq', 'head'))
The draws below stay inside these ranges and needn't reach their ends.
Inputs may be any that keep to these rules, and one draw needn't show every extreme that they name: `block_lists`: row g names block g first; all its entries lie within 16 blocks of the range of 32 blocks holding g: from max(0, (g // 32) * 32 - 16) to min(256, (g // 32 + 1) * 32 + 16) - 1, and both ends are named in every range that has them.
All inputs are finite; a program needn't handle non-finite values.
Results may differ from the reference program's by a relative error of at most 0.007.
The reference program's roundings to bfloat16 on the way (of `normed`, `weights`, `attended`, `features` and `buffer`) count: a program that leaves them out, or rounds other values in their place, can miss the bound.
Values may be sent and summed in bfloat16 or wider, within the bound.
A program may use at most 128 MiB of HBM per device.

```python
import math
import jax
import jax.numpy as jnp
from jax import lax

D = 1024
HEADS = 16
HD = 64
C = 128
BLK = 64
KB = 8
TAPS = 27
TOK_DEV = 512
NB_DEV = 8
GB = 32
HB = 16
FACE = 128
TOKENS = 16384
NBLOCKS = 256
N_SEQ = 8
DEVICES = 32


def draw_query_gain(key, part):
    folded = jax.random.fold_in(key, 11)
    lowest, highest = (math.log(0.5), math.log(2.0))
    return jnp.exp(jax.random.uniform(folded, (D,), jnp.float32, lowest, highest))


def draw_key_gain(key, part):
    folded = jax.random.fold_in(key, 12)
    lowest, highest = (math.log(0.5), math.log(2.0))
    return jnp.exp(jax.random.uniform(folded, (D,), jnp.float32, lowest, highest))


def draw_block_lists(key, part):
    folded = jax.random.fold_in(key, 21)
    block_ids = jnp.arange(NBLOCKS, dtype=jnp.int32)
    ranges = block_ids // GB
    lowest = jnp.maximum(ranges * GB - HB, 0)
    highest = jnp.minimum((ranges + 1) * GB + HB, NBLOCKS)
    raw_picks = jax.random.randint(folded, (NBLOCKS, KB - 1), 0, 1 << 20, dtype=jnp.int32)
    picks = lowest[:, None] + raw_picks % (highest - lowest)[:, None]
    inside = block_ids % GB
    first_pick = jnp.where(inside == 0, lowest, jnp.where(inside == GB - 1, highest - 1, picks[:, 0]))
    picks = picks.at[:, 0].set(first_pick)
    return jnp.concatenate([block_ids[:, None], picks], axis=1).astype(jnp.int32)


def place_ends(array, own_key, smallest, top_value):
    longest = array.shape.index(max(array.shape))
    spots = []
    for shift in (0, 1):
        where = [jax.random.randint(jax.random.fold_in(own_key, axis), (), 0, length) for axis, length in enumerate(array.shape)]
        where[longest] = (where[longest] + shift) % array.shape[longest]
        spots.append(tuple(where))
    return array.at[spots[0]].set(smallest).at[spots[1]].set(top_value)


def steps_of(own_key, shape, pieces, smallest, largest):
    loudness = 1.0
    for dim, parts in pieces:
        steps = jax.random.uniform(jax.random.fold_in(jax.random.fold_in(own_key, 6), dim), (parts,), jnp.float32, smallest / len(pieces), largest / len(pieces))
        loudness = loudness * jnp.repeat(jnp.exp(steps), shape[dim] // parts).reshape((-1,) + (1,) * (len(shape) - 1 - dim))
    return loudness


def scatter_about(own_key, extent, width, bound, shards=(), held_as=jnp.bfloat16):
    result = jax.random.normal(own_key, extent, jnp.float32) * width
    if len(shards) > 0:
        result = steps_of(own_key, extent, shards, -0.22, 0.18) * result
    return jnp.clip(result, min=-bound, max=bound).astype(held_as)


def setup_inputs(seed: int = 0) -> dict:
    key_list = jax.random.split(jax.random.key(seed), 16)
    return {
        "tokens": scatter_about(key_list[0], (TOKENS, D), 1.0, 6.0, ((0, 32),)),
        "mod_shift": scatter_about(key_list[1], (D,), 0.5, 3.0, (), jnp.float32),
        "mod_scale": scatter_about(key_list[2], (D,), 0.5, 3.0, (), jnp.float32),
        "attn_gate": scatter_about(key_list[3], (D,), 1.0, 4.0, (), jnp.float32),
        "w_qkv": scatter_about(key_list[4], (D, 3 * D), D ** -0.5, 0.1875),
        "query_gain": draw_query_gain(jax.random.fold_in(key_list[15], 71), 0),
        "key_gain": draw_key_gain(jax.random.fold_in(key_list[15], 71), 0),
        "w_out": scatter_about(key_list[7], (D, D), D ** -0.5, 0.1875),
        "w_dec": scatter_about(key_list[8], (D, C), D ** -0.5, 0.1875),
        "conv_weight": scatter_about(key_list[9], (TAPS * C, C), (TAPS * C) ** -0.5, 0.109375),
        "block_lists": draw_block_lists(jax.random.fold_in(key_list[15], 71), 0),
        "active_blocks": place_ends(jax.random.randint(key_list[11], (DEVICES,), (NB_DEV + 1) // 2, NB_DEV + 1), jax.random.fold_in(key_list[11], 1), (NB_DEV + 1) // 2, NB_DEV).astype(jnp.int32),
        "to_next": place_ends(jax.random.randint(key_list[12], (DEVICES * FACE,), 0, TOK_DEV), jax.random.fold_in(key_list[12], 1), 0, TOK_DEV - 1).astype(jnp.int32),
        "to_prev": place_ends(jax.random.randint(key_list[13], (DEVICES * FACE,), 0, TOK_DEV), jax.random.fold_in(key_list[13], 1), 0, TOK_DEV - 1).astype(jnp.int32),
        "conv_table": place_ends(jax.random.randint(key_list[14], (TOKENS, TAPS), 0, TOK_DEV + 2 * FACE + 1), jax.random.fold_in(key_list[14], 1), 0, TOK_DEV + 2 * FACE).astype(jnp.int32),
    }


EPSILON = 1e-06
MASKED = -1000000000.0

def layer_norm(values, mod_shift, mod_scale):
    centre = lax.optimization_barrier(jnp.mean(values, axis=-1, keepdims=True))
    centred = values - centre
    spread = lax.optimization_barrier(jnp.mean(centred * centred, axis=-1, keepdims=True))
    return centred * lax.rsqrt(spread + EPSILON) * (1.0 + mod_scale) + mod_shift

def head_norm(values, gain_row):
    per_head = values.reshape(values.shape[0], -1, HD)
    scaling = lax.rsqrt(lax.optimization_barrier(jnp.mean(per_head * per_head, axis=-1, keepdims=True)) + EPSILON)
    return (per_head * scaling).reshape(values.shape) * gain_row

def project(token_rows, mod_shift, mod_scale, w_qkv, query_gain, key_gain):
    normed = layer_norm(token_rows.astype(jnp.float32), mod_shift, mod_scale).astype(jnp.bfloat16)
    projected = jnp.dot(normed, w_qkv, preferred_element_type=jnp.float32)
    queries = head_norm(projected[:, :D], query_gain).astype(jnp.bfloat16)
    key_part = head_norm(projected[:, D:2 * D], key_gain).astype(jnp.bfloat16)
    values = projected[:, 2 * D:].astype(jnp.bfloat16)
    return (queries, key_part, values)

def block_flags(block_ids, active_blocks):
    owners = block_ids // NB_DEV
    slot_index = block_ids % NB_DEV
    owner_ids = jnp.arange(active_blocks.shape[0], dtype=jnp.int32)
    counted = lax.optimization_barrier(jnp.sum(jnp.where(owners[..., None] == owner_ids, active_blocks, 0), axis=-1))
    return slot_index < counted

def attend(queries, key_rows, value_rows, live_keys):
    scores = jnp.einsum('bqhd,bkhd->bhqk', queries.astype(jnp.float32), key_rows.astype(jnp.float32)) * (1.0 / math.sqrt(HD))
    penalty = jnp.where(jnp.repeat(live_keys, BLK, axis=1), jnp.float32(0.0), jnp.float32(MASKED))
    scores = scores + penalty[:, None, None, :]
    highest = lax.optimization_barrier(jnp.max(scores, axis=-1, keepdims=True))
    raised = jnp.exp(scores - highest)
    weights = (raised / lax.optimization_barrier(jnp.sum(raised, axis=-1, keepdims=True))).astype(jnp.bfloat16)
    output = jnp.einsum('bhqk,bkhd->bqhd', weights.astype(jnp.float32), value_rows.astype(jnp.float32))
    return output.astype(jnp.bfloat16)

def reference(tokens, mod_shift, mod_scale, attn_gate, w_qkv, query_gain, key_gain, w_out, w_dec, conv_weight, block_lists, active_blocks, to_next, to_prev, conv_table):

    def project_group(group_rows):
        return project(group_rows, mod_shift, mod_scale, w_qkv, query_gain, key_gain)
    queries, key_part, values = lax.map(project_group, tokens.reshape(N_SEQ, GB * BLK, D))
    key_blocks = key_part.reshape(NBLOCKS, BLK, HEADS, HD)
    value_blocks = values.reshape(NBLOCKS, BLK, HEADS, HD)
    live_lists = block_flags(block_lists, active_blocks)

    def one_group(inputs):
        query_rows, lists, live_keys = inputs
        picked_keys = key_blocks[lists].reshape(GB, KB * BLK, HEADS, HD)
        picked_values = value_blocks[lists].reshape(GB, KB * BLK, HEADS, HD)
        return attend(query_rows.reshape(GB, BLK, HEADS, HD), picked_keys, picked_values, live_keys)
    attended = lax.map(one_group, (queries, block_lists.reshape(N_SEQ, GB, KB), live_lists.reshape(N_SEQ, GB, KB)))
    attended = attended.reshape(TOKENS, D)
    update = jnp.dot(attended, w_out, preferred_element_type=jnp.float32)
    residual = tokens.astype(jnp.float32) + attn_gate * update
    slot_ids = jnp.arange(TOKENS, dtype=jnp.int32)
    live_rows = slot_ids % TOK_DEV < active_blocks[slot_ids // TOK_DEV] * BLK
    block_out = jnp.where(live_rows[:, None], residual, jnp.float32(0.0)).astype(jnp.bfloat16)
    features = jnp.dot(block_out, w_dec, preferred_element_type=jnp.float32).astype(jnp.bfloat16)
    per_owner = features.reshape(DEVICES, TOK_DEV, C)
    sent_next = jnp.take_along_axis(per_owner, to_next.reshape(DEVICES, FACE)[:, :, None], axis=1)
    sent_prev = jnp.take_along_axis(per_owner, to_prev.reshape(DEVICES, FACE)[:, :, None], axis=1)
    blank_rows = jnp.zeros((1, FACE, C), jnp.bfloat16)
    from_prev = jnp.concatenate([blank_rows, sent_next[:-1]], axis=0)
    from_next = jnp.concatenate([sent_prev[1:], blank_rows], axis=0)
    buffers = jnp.concatenate([per_owner, from_prev, from_next, jnp.zeros((DEVICES, 1, C), jnp.bfloat16)], axis=1)

    def convolve(inputs):
        buffer, offsets = inputs
        tap_rows = buffer[offsets].reshape(TOK_DEV, TAPS * C)
        return jnp.dot(tap_rows, conv_weight, preferred_element_type=jnp.float32)
    conv_out = lax.map(convolve, (buffers, conv_table.reshape(DEVICES, TOK_DEV, TAPS))).reshape(TOKENS, C)
    decoded = jnp.where(live_rows[:, None], features.astype(jnp.float32) + conv_out, jnp.float32(0.0)).astype(jnp.bfloat16)
    return (block_out, decoded)
```

```python
import functools
import math

import jax
import jax.numpy as jnp
from jax import lax
from jax.experimental import pallas as pl
from jax.experimental.pallas import tpu as pltpu
from jax.sharding import PartitionSpec as P

HD = 64
BLK = 64
NB = 8
KB = 8
EPSILON = 1e-06
MASKED = -1000000000.0
MESH = pl.DeviceIdType.MESH
BF16 = jnp.bfloat16
F32 = jnp.float32


def project_kernel(
    S, H,
    tokens, mod_shift, mod_scale, w_qkv, q_gain, k_gain,
    q, kv,
    normed, kv_send, q_send, own_sem,
    kv_ssem, kv_rsem, f_ssem, q_ssem, q_rsem,
):
    T, D = tokens.shape
    W = D // H
    half = H // 2
    s = lax.axis_index("seq")
    h = lax.axis_index("head")

    def peer_of(i):
        return ((h // 2 + i // 2) % half) * 2 + (h % 2 + i % 2) % 2

    has_next, has_prev = s < S - 1, s > 0

    barrier = pltpu.get_barrier_semaphore()
    for i in range(1, H):
        pl.semaphore_signal(barrier, inc=1, device_id=(s, peer_of(i)), device_id_type=MESH)
    for cond, where in ((has_next, (s + 1, h)), (has_prev, (s - 1, h))):
        @pl.when(cond)
        def _():
            pl.semaphore_signal(barrier, inc=1, device_id=where, device_id_type=MESH)

    RT = 64

    def norm_rows(r, _):
        rows = pl.ds(pl.multiple_of(r * RT, RT), RT)
        x = tokens[rows, :].astype(F32)
        centred = x - jnp.mean(x, axis=-1, keepdims=True)
        spread = jnp.mean(centred * centred, axis=-1, keepdims=True)
        y = centred * lax.rsqrt(spread + EPSILON) * (1.0 + mod_scale[...]) + mod_shift[...]
        normed[rows, :] = y.astype(BF16)
        return 0

    lax.fori_loop(0, T // RT, norm_rows, 0)

    pl.semaphore_wait(
        barrier, H - 1 + jnp.where(has_next, jnp.int32(1), jnp.int32(0)) + jnp.where(has_prev, jnp.int32(1), jnp.int32(0))
    )

    same = (
        lax.broadcasted_iota(jnp.int32, (W, W), 0) // HD
        == lax.broadcasted_iota(jnp.int32, (W, W), 1) // HD
    )
    averaging = jnp.where(same, F32(1.0 / HD), F32(0.0)).astype(BF16)

    def head_norm(x, gain):
        square = x * x
        high = square.astype(BF16)
        low = (square - high.astype(F32)).astype(BF16)
        mean = jnp.dot(high, averaging, preferred_element_type=F32) + jnp.dot(
            low, averaging, preferred_element_type=F32
        )
        return (x * lax.rsqrt(mean + EPSILON) * gain).astype(BF16)

    PT = min(256, T)

    def columns(part, owner):
        return pl.ds(pl.multiple_of(part * D + owner * W, W), W)

    def gains(ref, owner):
        return ref[:, pl.ds(pl.multiple_of(owner * W, W), W)]

    def make_kv(dst, slot, owner):
        def step(r, _):
            rows = pl.ds(pl.multiple_of(r * PT, PT), PT)
            x = normed[rows, :]
            key = jnp.dot(x, w_qkv[:, columns(1, owner)], preferred_element_type=F32)
            dst[slot, rows, 0:W] = head_norm(key, gains(k_gain, owner))
            val = jnp.dot(x, w_qkv[:, columns(2, owner)], preferred_element_type=F32)
            dst[slot, rows, W : 2 * W] = val.astype(BF16)
            return 0

        lax.fori_loop(0, T // PT, step, 0)

    def make_q(dst, slot, owner):
        def step(r, _):
            rows = pl.ds(pl.multiple_of(r * PT, PT), PT)
            x = jnp.dot(normed[rows, :], w_qkv[:, columns(0, owner)], preferred_element_type=F32)
            dst[slot, rows, :] = head_norm(x, gains(q_gain, owner))
            return 0

        lax.fori_loop(0, T // PT, step, 0)

    def kv_copy(i):
        return pltpu.make_async_remote_copy(
            src_ref=kv_send.at[i],
            dst_ref=kv.at[half + h],
            send_sem=kv_ssem.at[i],
            recv_sem=kv_rsem.at[half + h],
            device_id=(s, peer_of(i)),
            device_id_type=MESH,
        )

    def q_copy(i):
        return pltpu.make_async_remote_copy(
            src_ref=q_send.at[i],
            dst_ref=q.at[h],
            send_sem=q_ssem.at[i],
            recv_sem=q_rsem.at[h],
            device_id=(s, peer_of(i)),
            device_id_type=MESH,
        )

    def forward_copy(i, slot, target):
        return pltpu.make_async_remote_copy(
            src_ref=kv_send.at[0] if i == 0 else kv.at[half + peer_of(i)],
            dst_ref=kv.at[slot],
            send_sem=f_ssem.at[i],
            recv_sem=kv_rsem.at[slot],
            device_id=(target, h),
            device_id_type=MESH,
        )

    def each_forward(i, act):
        owner = peer_of(i)

        @pl.when(jnp.logical_and(owner >= half, has_next))
        def _():
            act(forward_copy(i, owner - half, s + 1))

        @pl.when(jnp.logical_and(owner < half, has_prev))
        def _():
            act(forward_copy(i, half + H + owner, s - 1))

    def kv_arrival(slot):
        pltpu.make_async_copy(kv.at[slot], kv.at[slot], kv_rsem.at[slot]).wait()

    own_kv = pltpu.make_async_copy(kv_send.at[0], kv.at[half + h], own_sem.at[0])
    own_q = pltpu.make_async_copy(q_send.at[0], q.at[h], own_sem.at[1])
    order = list(range(2, H)) + [1]
    make_kv(kv_send, 0, h)
    each_forward(0, lambda c: c.start())
    own_kv.start()
    for i in order:
        make_kv(kv_send, i, peer_of(i))
        kv_copy(i).start()
    kv_arrival(half + peer_of(1))
    each_forward(1, lambda c: c.start())
    for i in order:
        make_q(q_send, i, peer_of(i))
        q_copy(i).start()
    make_q(q_send, 0, h)
    own_q.start()
    for i in range(2, H):
        kv_arrival(half + peer_of(i))
        each_forward(i, lambda c: c.start())
    for i in range(1, H):
        pltpu.make_async_copy(q.at[peer_of(i)], q.at[peer_of(i)], q_rsem.at[peer_of(i)]).wait()
    for j in range(half):
        @pl.when(has_prev)
        def _():
            kv_arrival(j)

        @pl.when(has_next)
        def _():
            kv_arrival(half + H + j)

    own_kv.wait()
    own_q.wait()
    for i in range(1, H):
        kv_copy(i).wait_send()
        q_copy(i).wait_send()
    for i in range(H):
        each_forward(i, lambda c: c.wait_send())


def attend_kernel(lists, active, q, kv, o):
    H, T, W = q.shape
    heads = W // HD
    group = lax.axis_index("seq") * H
    o[...] = jnp.zeros_like(o)
    rows_of = lax.broadcasted_iota(jnp.int32, (heads * BLK, W), 0) // BLK
    lanes_of = lax.broadcasted_iota(jnp.int32, (heads * BLK, W), 1) // HD
    diagonal = jnp.where(rows_of == lanes_of, F32(1.0 / math.sqrt(HD)), F32(0.0)).astype(BF16)
    block_of = lax.broadcasted_iota(jnp.int32, (1, KB * BLK), 1) // BLK
    lane_head = lax.broadcasted_iota(jnp.int32, (BLK, W), 1) // HD
    base = (lax.axis_index("seq") * H - H // 2) * NB

    def attend(owner, b):
        rows = pl.ds(pl.multiple_of(b * BLK, BLK), BLK)
        query = q[owner, rows, :]
        spread = jnp.concatenate([query] * heads, axis=0) * diagonal
        keys, values = [], []
        penalty = jnp.zeros((1, KB * BLK), F32)
        for n in range(KB):
            block = lists[owner * NB + b, n]
            live = lax.rem(block, NB) < active[block // NB]
            penalty = jnp.where(
                block_of == n, jnp.where(live, F32(0.0), F32(MASKED)), penalty
            )
            local = block - base
            keys.append(kv[local, :, 0:W])
            values.append(kv[local, :, W : 2 * W])
        scores = lax.dot_general(
            spread, jnp.concatenate(keys, axis=0), (((1,), (1,)), ((), ())),
            preferred_element_type=F32,
        ) + penalty
        raised = jnp.exp(scores - jnp.max(scores, axis=-1, keepdims=True))
        weights = (raised * (1.0 / jnp.sum(raised, axis=-1, keepdims=True))).astype(BF16)
        mixed = jnp.dot(weights, jnp.concatenate(values, axis=0), preferred_element_type=F32)
        result = mixed[0:BLK, :]
        for n in range(1, heads):
            result = jnp.where(lane_head == n, mixed[n * BLK : (n + 1) * BLK, :], result)
        o[owner, rows, :] = result.astype(BF16)

    def each_owner(owner, _):
        def pair(b, _):
            attend(owner, 2 * b)
            attend(owner, 2 * b + 1)
            return 0

        return lax.fori_loop(0, (active[group + owner] + 1) // 2, pair, 0)

    lax.fori_loop(0, H, each_owner, 0)


def finish_kernel(
    S, H,
    tokens, attn_gate, o, w_out, w_dec, conv_w, active, to_next, to_prev, table,
    block_out, decoded,
    att, acc, onehot, buf, face, own_sem, o_ssem, o_rsem, face_ssem, face_rsem,
):
    T, D = tokens.shape
    W = D // H
    C = w_dec.shape[1]
    TAPS = table.shape[1]
    FACE = to_next.shape[0]
    half = H // 2
    RT = 64
    s = lax.axis_index("seq")
    h = lax.axis_index("head")

    def peer_of(i):
        return ((h // 2 + i // 2) % half) * 2 + (h % 2 + i % 2) % 2

    has_next, has_prev = s < S - 1, s > 0
    wrap_next = jnp.logical_and(h == H - 1, has_next)
    wrap_prev = jnp.logical_and(h == 0, has_prev)

    barrier = pltpu.get_barrier_semaphore()
    for i in range(1, H):
        pl.semaphore_signal(barrier, inc=1, device_id=(s, peer_of(i)), device_id_type=MESH)
    for cond, where in ((wrap_next, (s + 1, 0)), (wrap_prev, (s - 1, H - 1))):
        @pl.when(cond)
        def _():
            pl.semaphore_signal(barrier, inc=1, device_id=where, device_id_type=MESH)
    pl.semaphore_wait(
        barrier, H - 1 + jnp.where(wrap_next, jnp.int32(1), jnp.int32(0)) + jnp.where(wrap_prev, jnp.int32(1), jnp.int32(0))
    )

    def o_copy(i):
        return pltpu.make_async_remote_copy(
            src_ref=o.at[peer_of(i)],
            dst_ref=att.at[h],
            send_sem=o_ssem.at[i],
            recv_sem=o_rsem.at[h],
            device_id=(s, peer_of(i)),
            device_id_type=MESH,
        )

    own_o = pltpu.make_async_copy(o.at[h], att.at[h], own_sem)
    for i in list(range(2, H)) + [1]:
        o_copy(i).start()
    own_o.start()

    spots = lax.broadcasted_iota(jnp.int32, (T, T + 2 * FACE), 1).astype(F32)
    tap_lane = lax.broadcasted_iota(jnp.int32, (T, TAPS), 1)

    def build(t, _):
        want = jnp.sum(jnp.where(tap_lane == t, table[...].astype(F32), 0.0), axis=1, keepdims=True)
        onehot[t] = jnp.where(spots == want, F32(1.0), F32(0.0)).astype(BF16)
        return 0

    lax.fori_loop(0, TAPS, build, 0)

    def add_out(value, owner, first):
        part = jnp.dot(
            value, w_out[pl.ds(pl.multiple_of(owner * W, W), W), :], preferred_element_type=F32
        )
        acc[...] = part if first else acc[...] + part

    own_o.wait()
    add_out(att[h], h, True)
    for i in range(1, H):
        owner = peer_of(i)
        pltpu.make_async_copy(att.at[owner], att.at[owner], o_rsem.at[owner]).wait()
        add_out(att[owner], owner, False)

    own_live = active[s * H + h] * BLK

    def finish(r, _):
        rows = pl.ds(pl.multiple_of(r * RT, RT), RT)
        live = lax.broadcasted_iota(jnp.int32, (RT, 1), 0) + r * RT < own_live
        residual = tokens[rows, :].astype(F32) + attn_gate[...] * acc[rows, :]
        block_out[rows, :] = jnp.where(live, residual, 0.0).astype(BF16)
        return 0

    lax.fori_loop(0, T // RT, finish, 0)
    features = jnp.dot(block_out[...], w_dec[...], preferred_element_type=F32).astype(BF16)
    buf[0:T, :] = features

    slots = lax.broadcasted_iota(jnp.int32, (FACE, T), 1)
    for n, ref in enumerate((to_next, to_prev)):
        chosen = jnp.where(slots == ref[...], F32(1.0), F32(0.0)).astype(BF16)
        face[n] = jnp.dot(chosen, features, preferred_element_type=F32).astype(BF16)

    def face_copy(n, target):
        return pltpu.make_async_remote_copy(
            src_ref=face.at[n],
            dst_ref=buf.at[pl.ds(T + n * FACE, FACE), :],
            send_sem=face_ssem.at[n],
            recv_sem=face_rsem.at[n],
            device_id=target,
            device_id_type=MESH,
        )

    any_next = jnp.logical_or(has_next, h < H - 1)
    any_prev = jnp.logical_or(has_prev, h > 0)
    device = s * H + h

    @pl.when(any_next)
    def _():
        face_copy(0, ((device + 1) // H, (device + 1) % H)).start()

    @pl.when(any_prev)
    def _():
        face_copy(1, ((device - 1) // H, (device - 1) % H)).start()

    def face_arrival(n):
        rows = buf.at[pl.ds(T + n * FACE, FACE), :]
        pltpu.make_async_copy(rows, rows, face_rsem.at[n]).wait()

    for n, cond in ((0, any_prev), (1, any_next)):
        @pl.when(cond)
        def _():
            face_arrival(n)

        @pl.when(jnp.logical_not(cond))
        def _():
            buf[T + n * FACE : T + (n + 1) * FACE, :] = jnp.zeros((FACE, C), BF16)

    def tap(t, total):
        rows = jnp.dot(onehot[t], buf[...], preferred_element_type=F32).astype(BF16)
        return total + jnp.dot(rows, conv_w[t], preferred_element_type=F32)

    total = lax.fori_loop(0, TAPS, tap, buf[0:T, :].astype(F32))
    live = lax.broadcasted_iota(jnp.int32, (T, 1), 0) < own_live
    decoded[...] = jnp.where(live, total, 0.0).astype(BF16)

    for i in range(1, H):
        o_copy(i).wait_send()

    @pl.when(any_next)
    def _():
        face_copy(0, ((device + 1) // H, (device + 1) % H)).wait_send()

    @pl.when(any_prev)
    def _():
        face_copy(1, ((device - 1) // H, (device - 1) % H)).wait_send()


def body(
    tokens, mod_shift, mod_scale, attn_gate, w_qkv, query_gain, key_gain, w_out, w_dec,
    conv_weight, block_lists, active_blocks, to_next, to_prev, conv_table,
):
    S, H = lax.axis_size("seq"), lax.axis_size("head")
    T, D = tokens.shape
    W = D // H
    C = w_dec.shape[1]
    taps = conv_table.shape[1]
    face = to_next.shape[0]
    vmem = pl.BlockSpec(memory_space=pltpu.VMEM)
    smem = pl.BlockSpec(memory_space=pltpu.SMEM)
    hbm = pl.BlockSpec(memory_space=pl.ANY)
    dma = pltpu.SemaphoreType.DMA
    grant = 60 * 1024 * 1024
    q, kv = pl.pallas_call(
        functools.partial(project_kernel, S, H),
        out_shape=(
            jax.ShapeDtypeStruct((H, T, W), BF16),
            jax.ShapeDtypeStruct((2 * H, T, 2 * W), BF16),
        ),
        in_specs=[vmem] * 6,
        out_specs=(hbm, hbm),
        scratch_shapes=[
            pltpu.VMEM((T, D), BF16),
            pltpu.VMEM((H, T, 2 * W), BF16),
            pltpu.VMEM((H, T, W), BF16),
            dma((2,)),
            dma((H,)), dma((2 * H,)), dma((H,)),
            dma((H,)), dma((H,)),
        ],
        compiler_params=pltpu.CompilerParams(
            collective_id=0, has_side_effects=True, vmem_limit_bytes=grant
        ),
    )(
        tokens, mod_shift.reshape(1, D), mod_scale.reshape(1, D), w_qkv,
        query_gain.reshape(1, D), key_gain.reshape(1, D),
    )
    o = pl.pallas_call(
        attend_kernel,
        out_shape=jax.ShapeDtypeStruct((H, T, W), BF16),
        in_specs=[smem, smem, vmem, vmem],
        out_specs=vmem,
        compiler_params=pltpu.CompilerParams(vmem_limit_bytes=grant),
    )(block_lists, active_blocks, q, kv.reshape(2 * H * NB, BLK, 2 * W))
    return pl.pallas_call(
        functools.partial(finish_kernel, S, H),
        out_shape=(
            jax.ShapeDtypeStruct((T, D), BF16),
            jax.ShapeDtypeStruct((T, C), BF16),
        ),
        in_specs=[vmem, vmem, hbm, vmem, vmem, vmem, smem, vmem, vmem, vmem],
        out_specs=(vmem, vmem),
        scratch_shapes=[
            pltpu.VMEM((H, T, W), BF16),
            pltpu.VMEM((T, D), F32),
            pltpu.VMEM((taps, T, T + 2 * face), BF16),
            pltpu.VMEM((T + 2 * face, C), BF16),
            pltpu.VMEM((2, face, C), BF16),
            dma, dma((H,)), dma((H,)), dma((2,)), dma((2,)),
        ],
        compiler_params=pltpu.CompilerParams(
            collective_id=1, has_side_effects=True, vmem_limit_bytes=grant
        ),
    )(
        tokens, attn_gate.reshape(1, D), o, w_out, w_dec, conv_weight.reshape(taps, C, C),
        active_blocks, to_next.reshape(face, 1), to_prev.reshape(face, 1), conv_table,
    )


def solution(mesh):
    rows = P(("seq", "head"), None)
    return jax.shard_map(
        body,
        mesh=mesh,
        in_specs=(
            rows, P(), P(), P(), P(), P(), P(), P(), P(), P(),
            P("seq", None), P(), P(("seq", "head")), P(("seq", "head")), rows,
        ),
        out_specs=(rows, rows),
        check_vma=False,
    )
```

```python
import functools
import math

import jax
import jax.numpy as jnp
from jax import lax
from jax.experimental import pallas as pl
from jax.experimental.pallas import tpu as pltpu
from jax.sharding import PartitionSpec as P

HD = 64
BLK = 64
NB = 8
KB = 8
EPSILON = 1e-06
MASKED = -1000000000.0
MESH = pl.DeviceIdType.MESH
BF16 = jnp.bfloat16
F32 = jnp.float32


class Group:
    def __init__(self, P, H):
        self.s, self.h = lax.axis_index("seq"), lax.axis_index("head")
        self.P, self.H, self.G, self.half = P, H, P * H, H // 2
        self.chips = self.G // 2
        self.first = self.s - self.s % P
        self.me = (self.s % P) * H + self.h
        self.chip, self.core = self.me // 2, self.me % 2
        self.others = [(0, 1)] + [(i, k) for i in range(1, self.chips) for k in range(2)]

    def chip_at(self, i):
        return (self.chip + i) % self.chips

    def core_at(self, k):
        return (self.core + k) % 2

    def member(self, i, k):
        return self.chip_at(i) * 2 + self.core_at(k)

    def place(self, i, k):
        member = self.member(i, k)
        return (self.first + member // self.H, member % self.H)


def ranges_per_group(S, H, D):
    return 2 if S % 2 == 0 and D // (2 * H) % 128 == 0 else 1


def project_kernel(
    S, H, P,
    tokens, mod_shift, mod_scale, w_qkv, q_gain, k_gain, lists,
    q, kv, all_lists,
    normed, kv_send, q_send, own_sem, list_ssem, list_rsem,
    kv_ssem, kv_rsem, f_ssem, q_ssem, q_rsem,
):
    T, D = tokens.shape
    g = Group(P, H)
    s, h, G, half = g.s, g.h, g.G, g.half
    W = D // G
    WIDE = 2 * W
    has_next, has_prev = g.first + P < S, g.first > 0

    barrier = pltpu.get_barrier_semaphore()
    for i, k in g.others:
        pl.semaphore_signal(barrier, inc=1, device_id=g.place(i, k), device_id_type=MESH)
    for cond, where in ((has_next, (s + P, h)), (has_prev, (s - P, h))):
        @pl.when(cond)
        def _():
            pl.semaphore_signal(barrier, inc=1, device_id=where, device_id_type=MESH)

    RT = 64

    def norm_rows(r, _):
        rows = pl.ds(pl.multiple_of(r * RT, RT), RT)
        x = tokens[rows, :].astype(F32)
        centred = x - jnp.mean(x, axis=-1, keepdims=True)
        spread = jnp.mean(centred * centred, axis=-1, keepdims=True)
        y = centred * lax.rsqrt(spread + EPSILON) * (1.0 + mod_scale[...]) + mod_shift[...]
        normed[rows, :] = y.astype(BF16)
        return 0

    lax.fori_loop(0, T // RT, norm_rows, 0)

    pl.semaphore_wait(
        barrier, G - 1 + jnp.where(has_next, jnp.int32(1), jnp.int32(0)) + jnp.where(has_prev, jnp.int32(1), jnp.int32(0))
    )

    same = (
        lax.broadcasted_iota(jnp.int32, (WIDE, WIDE), 0) // HD
        == lax.broadcasted_iota(jnp.int32, (WIDE, WIDE), 1) // HD
    )
    averaging = jnp.where(same, F32(1.0 / HD), F32(0.0)).astype(BF16)

    def head_norm(x, gain):
        square = x * x
        high = square.astype(BF16)
        low = (square - high.astype(F32)).astype(BF16)
        mean = jnp.dot(high, averaging, preferred_element_type=F32) + jnp.dot(
            low, averaging, preferred_element_type=F32
        )
        return (x * lax.rsqrt(mean + EPSILON) * gain).astype(BF16)

    PT = min(256, T)

    def columns(part, i):
        return pl.ds(pl.multiple_of(part * D + g.chip_at(i) * WIDE, WIDE), WIDE)

    def make_kv(i):
        def step(r, _):
            rows = pl.ds(pl.multiple_of(r * PT, PT), PT)
            x = normed[rows, :]
            key = jnp.dot(x, w_qkv[:, columns(1, i)], preferred_element_type=F32)
            key = head_norm(key, k_gain[:, columns(0, i)])
            val = jnp.dot(x, w_qkv[:, columns(2, i)], preferred_element_type=F32).astype(BF16)
            for core in range(2):
                kv_send[2 * i + core, rows, 0:W] = key[:, core * W : (core + 1) * W]
                kv_send[2 * i + core, rows, W : 2 * W] = val[:, core * W : (core + 1) * W]
            return 0

        lax.fori_loop(0, T // PT, step, 0)

    def make_q(i):
        def step(r, _):
            rows = pl.ds(pl.multiple_of(r * PT, PT), PT)
            x = jnp.dot(normed[rows, :], w_qkv[:, columns(0, i)], preferred_element_type=F32)
            x = head_norm(x, q_gain[:, columns(0, i)])
            for core in range(2):
                q_send[2 * i + core, rows, :] = x[:, core * W : (core + 1) * W]
            return 0

        lax.fori_loop(0, T // PT, step, 0)

    def kv_copy(i, k):
        return pltpu.make_async_remote_copy(
            src_ref=kv_send.at[2 * i + g.core_at(k)],
            dst_ref=kv.at[half + g.me],
            send_sem=kv_ssem.at[2 * i + k],
            recv_sem=kv_rsem.at[half + g.me],
            device_id=g.place(i, k),
            device_id_type=MESH,
        )

    def q_copy(i, k):
        return pltpu.make_async_remote_copy(
            src_ref=q_send.at[2 * i + g.core_at(k)],
            dst_ref=q.at[g.me],
            send_sem=q_ssem.at[2 * i + k],
            recv_sem=q_rsem.at[g.me],
            device_id=g.place(i, k),
            device_id_type=MESH,
        )

    def list_copy(n):
        return pltpu.make_async_remote_copy(
            src_ref=lists,
            dst_ref=all_lists.at[s % P],
            send_sem=list_ssem.at[n],
            recv_sem=list_rsem.at[s % P],
            device_id=(g.first + (s + n) % P, h),
            device_id_type=MESH,
        )

    def forward_copy(i, k, slot, target):
        own = (i, k) == (0, 0)
        return pltpu.make_async_remote_copy(
            src_ref=kv_send.at[g.core] if own else kv.at[half + g.member(i, k)],
            dst_ref=kv.at[slot],
            send_sem=f_ssem.at[2 * i + k],
            recv_sem=kv_rsem.at[slot],
            device_id=(target, h),
            device_id_type=MESH,
        )

    def each_forward(i, k, act):
        owner = g.member(i, k)

        @pl.when(jnp.logical_and(owner >= G - half, has_next))
        def _():
            act(forward_copy(i, k, owner - (G - half), s + P))

        @pl.when(jnp.logical_and(owner < half, has_prev))
        def _():
            act(forward_copy(i, k, half + G + owner, s - P))

    def arrival(ref, slot, sem):
        pltpu.make_async_copy(ref.at[slot], ref.at[slot], sem.at[slot]).wait()

    own_kv = pltpu.make_async_copy(kv_send.at[g.core], kv.at[half + g.me], own_sem.at[0])
    own_q = pltpu.make_async_copy(q_send.at[g.core], q.at[g.me], own_sem.at[1])
    own_list = pltpu.make_async_copy(lists, all_lists.at[s % P], own_sem.at[2])
    own_list.start()
    for n in range(1, P):
        list_copy(n).start()
    for i in list(range(1, g.chips)) + [0]:
        make_kv(i)
        for k in range(2) if i else (1,):
            kv_copy(i, k).start()
    each_forward(0, 0, lambda c: c.start())
    own_kv.start()
    for i in list(range(1, g.chips)) + [0]:
        make_q(i)
        for k in range(2) if i else (1,):
            q_copy(i, k).start()
    own_q.start()
    for i, k in [(0, 1)] + g.others[:0:-1]:
        arrival(kv, half + g.member(i, k), kv_rsem)
        each_forward(i, k, lambda c: c.start())
    for i, k in g.others:
        arrival(q, g.member(i, k), q_rsem)
    for n in range(1, P):
        arrival(all_lists, (s + n) % P, list_rsem)
    for j in range(half):
        @pl.when(has_prev)
        def _():
            arrival(kv, j, kv_rsem)

        @pl.when(has_next)
        def _():
            arrival(kv, half + G + j, kv_rsem)

    own_kv.wait()
    own_q.wait()
    own_list.wait()
    for n in range(1, P):
        list_copy(n).wait_send()
    for i, k in g.others:
        kv_copy(i, k).wait_send()
        q_copy(i, k).wait_send()
    for i, k in [(0, 0)] + g.others:
        each_forward(i, k, lambda c: c.wait_send())


def attend_kernel(half, P, lists, active, q, kv, o):
    G, T, W = q.shape
    heads = W // HD
    group = (lax.axis_index("seq") // P) * G
    o[...] = jnp.zeros_like(o)
    rows_of = lax.broadcasted_iota(jnp.int32, (heads * BLK, W), 0) // BLK
    lanes_of = lax.broadcasted_iota(jnp.int32, (heads * BLK, W), 1) // HD
    diagonal = jnp.where(rows_of == lanes_of, F32(1.0 / math.sqrt(HD)), F32(0.0)).astype(BF16)
    block_of = lax.broadcasted_iota(jnp.int32, (1, KB * BLK), 1) // BLK
    lane_head = lax.broadcasted_iota(jnp.int32, (BLK, W), 1) // HD
    base = (group - half) * NB

    def attend(owner, b):
        rows = pl.ds(pl.multiple_of(b * BLK, BLK), BLK)
        query = q[owner, rows, :]
        spread = jnp.concatenate([query] * heads, axis=0) * diagonal
        keys, values = [], []
        penalty = jnp.zeros((1, KB * BLK), F32)
        for n in range(KB):
            block = lists[owner * NB + b, n]
            live = lax.rem(block, NB) < active[block // NB]
            penalty = jnp.where(
                block_of == n, jnp.where(live, F32(0.0), F32(MASKED)), penalty
            )
            local = block - base
            keys.append(kv[local, :, 0:W])
            values.append(kv[local, :, W : 2 * W])
        scores = lax.dot_general(
            spread, jnp.concatenate(keys, axis=0), (((1,), (1,)), ((), ())),
            preferred_element_type=F32,
        ) + penalty
        raised = jnp.exp(scores - jnp.max(scores, axis=-1, keepdims=True))
        weights = (raised * (1.0 / jnp.sum(raised, axis=-1, keepdims=True))).astype(BF16)
        mixed = jnp.dot(weights, jnp.concatenate(values, axis=0), preferred_element_type=F32)
        result = mixed[0:BLK, :]
        for n in range(1, heads):
            result = jnp.where(lane_head == n, mixed[n * BLK : (n + 1) * BLK, :], result)
        o[owner, rows, :] = result.astype(BF16)

    def each_owner(owner, _):
        def pair(b, _):
            attend(owner, 2 * b)
            attend(owner, 2 * b + 1)
            return 0

        return lax.fori_loop(0, (active[group + owner] + 1) // 2, pair, 0)

    lax.fori_loop(0, G, each_owner, 0)


def finish_kernel(
    S, H, P,
    tokens, attn_gate, o, w_out, w_dec, conv_w, active, to_next, to_prev, table,
    block_out, decoded,
    att, acc, onehot, buf, face, own_sem, o_ssem, o_rsem, face_ssem, face_rsem,
):
    T, D = tokens.shape
    C = w_dec.shape[1]
    TAPS = table.shape[1]
    FACE = to_next.shape[1]
    RT = 64
    g = Group(P, H)
    s, h, G = g.s, g.h, g.G
    W = D // G
    has_next, has_prev = s < S - 1, s > 0
    wrap_next = jnp.logical_and(g.me == G - 1, has_next)
    wrap_prev = jnp.logical_and(g.me == 0, has_prev)

    barrier = pltpu.get_barrier_semaphore()
    for i, k in g.others:
        pl.semaphore_signal(barrier, inc=1, device_id=g.place(i, k), device_id_type=MESH)
    for cond, where in ((wrap_next, (s + 1, 0)), (wrap_prev, (s - 1, H - 1))):
        @pl.when(cond)
        def _():
            pl.semaphore_signal(barrier, inc=1, device_id=where, device_id_type=MESH)
    pl.semaphore_wait(
        barrier, G - 1 + jnp.where(wrap_next, jnp.int32(1), jnp.int32(0)) + jnp.where(wrap_prev, jnp.int32(1), jnp.int32(0))
    )

    def o_copy(i, k):
        return pltpu.make_async_remote_copy(
            src_ref=o.at[g.member(i, k)],
            dst_ref=att.at[g.me],
            send_sem=o_ssem.at[2 * i + k],
            recv_sem=o_rsem.at[g.me],
            device_id=g.place(i, k),
            device_id_type=MESH,
        )

    own_o = pltpu.make_async_copy(o.at[g.me], att.at[g.me], own_sem)
    for i, k in g.others[::-1]:
        o_copy(i, k).start()
    own_o.start()

    spots = lax.broadcasted_iota(jnp.int32, (T, T + 2 * FACE), 1).astype(F32)
    tap_lane = lax.broadcasted_iota(jnp.int32, (T, TAPS), 1)

    def build(t, _):
        want = jnp.sum(jnp.where(tap_lane == t, table[...].astype(F32), 0.0), axis=1, keepdims=True)
        onehot[t] = jnp.where(spots == want, F32(1.0), F32(0.0)).astype(BF16)
        return 0

    lax.fori_loop(0, TAPS, build, 0)

    own_o.wait()
    for i, k in g.others:
        owner = g.member(i, k)
        pltpu.make_async_copy(att.at[owner], att.at[owner], o_rsem.at[owner]).wait()
    attended = jnp.concatenate([att[n] for n in range(G)], axis=1)
    acc[...] = jnp.dot(attended, w_out[...], preferred_element_type=F32)

    own_live = active[s * H + h] * BLK

    def finish(r, _):
        rows = pl.ds(pl.multiple_of(r * RT, RT), RT)
        live = lax.broadcasted_iota(jnp.int32, (RT, 1), 0) + r * RT < own_live
        residual = tokens[rows, :].astype(F32) + attn_gate[...] * acc[rows, :]
        block_out[rows, :] = jnp.where(live, residual, 0.0).astype(BF16)
        return 0

    lax.fori_loop(0, T // RT, finish, 0)
    features = jnp.dot(block_out[...], w_dec[...], preferred_element_type=F32).astype(BF16)
    buf[0:T, :] = features

    slots = lax.broadcasted_iota(jnp.int32, (T, FACE), 0)
    for n, ref in enumerate((to_next, to_prev)):
        chosen = jnp.where(slots == ref[...], F32(1.0), F32(0.0)).astype(BF16)
        face[n] = lax.dot_general(
            chosen, features, (((0,), (0,)), ((), ())), preferred_element_type=F32
        ).astype(BF16)

    def face_copy(n, target):
        return pltpu.make_async_remote_copy(
            src_ref=face.at[n],
            dst_ref=buf.at[pl.ds(T + n * FACE, FACE), :],
            send_sem=face_ssem.at[n],
            recv_sem=face_rsem.at[n],
            device_id=target,
            device_id_type=MESH,
        )

    any_next = jnp.logical_or(has_next, h < H - 1)
    any_prev = jnp.logical_or(has_prev, h > 0)
    device = s * H + h

    @pl.when(any_next)
    def _():
        face_copy(0, ((device + 1) // H, (device + 1) % H)).start()

    @pl.when(any_prev)
    def _():
        face_copy(1, ((device - 1) // H, (device - 1) % H)).start()

    def face_arrival(n):
        rows = buf.at[pl.ds(T + n * FACE, FACE), :]
        pltpu.make_async_copy(rows, rows, face_rsem.at[n]).wait()

    for n, cond in ((0, any_prev), (1, any_next)):
        @pl.when(cond)
        def _():
            face_arrival(n)

        @pl.when(jnp.logical_not(cond))
        def _():
            buf[T + n * FACE : T + (n + 1) * FACE, :] = jnp.zeros((FACE, C), BF16)

    def tap(t, total):
        rows = jnp.dot(onehot[t], buf[...], preferred_element_type=F32).astype(BF16)
        return total + jnp.dot(rows, conv_w[t], preferred_element_type=F32)

    total = lax.fori_loop(0, TAPS, tap, buf[0:T, :].astype(F32))
    live = lax.broadcasted_iota(jnp.int32, (T, 1), 0) < own_live
    decoded[...] = jnp.where(live, total, 0.0).astype(BF16)

    for i, k in g.others:
        o_copy(i, k).wait_send()

    @pl.when(any_next)
    def _():
        face_copy(0, ((device + 1) // H, (device + 1) % H)).wait_send()

    @pl.when(any_prev)
    def _():
        face_copy(1, ((device - 1) // H, (device - 1) % H)).wait_send()


def body(
    tokens, mod_shift, mod_scale, attn_gate, w_qkv, query_gain, key_gain, w_out, w_dec,
    conv_weight, block_lists, active_blocks, to_next, to_prev, conv_table,
):
    S, H = lax.axis_size("seq"), lax.axis_size("head")
    T, D = tokens.shape
    P = ranges_per_group(S, H, D)
    G = P * H
    W = D // G
    GB = block_lists.shape[0]
    C = w_dec.shape[1]
    taps = conv_table.shape[1]
    face = to_next.shape[0]
    vmem = pl.BlockSpec(memory_space=pltpu.VMEM)
    smem = pl.BlockSpec(memory_space=pltpu.SMEM)
    hbm = pl.BlockSpec(memory_space=pl.ANY)
    dma = pltpu.SemaphoreType.DMA
    grant = 60 * 1024 * 1024
    q, kv, lists = pl.pallas_call(
        functools.partial(project_kernel, S, H, P),
        out_shape=(
            jax.ShapeDtypeStruct((G, T, W), BF16),
            jax.ShapeDtypeStruct((G + H, T, 2 * W), BF16),
            jax.ShapeDtypeStruct((P,) + block_lists.shape, jnp.int32),
        ),
        in_specs=[vmem] * 6 + [hbm],
        out_specs=(hbm, hbm, hbm),
        scratch_shapes=[
            pltpu.VMEM((T, D), BF16),
            pltpu.VMEM((G, T, 2 * W), BF16),
            pltpu.VMEM((G, T, W), BF16),
            dma((3,)), dma((P,)), dma((P,)),
            dma((G,)), dma((G + H,)), dma((G,)),
            dma((G,)), dma((G,)),
        ],
        compiler_params=pltpu.CompilerParams(
            collective_id=0, has_side_effects=True, vmem_limit_bytes=grant
        ),
    )(
        tokens, mod_shift.reshape(1, D), mod_scale.reshape(1, D), w_qkv,
        query_gain.reshape(1, D), key_gain.reshape(1, D), block_lists,
    )
    o = pl.pallas_call(
        functools.partial(attend_kernel, H // 2, P),
        out_shape=jax.ShapeDtypeStruct((G, T, W), BF16),
        in_specs=[smem, smem, vmem, vmem],
        out_specs=vmem,
        compiler_params=pltpu.CompilerParams(vmem_limit_bytes=grant),
    )(lists.reshape(P * GB, KB), active_blocks, q, kv.reshape((G + H) * NB, BLK, 2 * W))
    return pl.pallas_call(
        functools.partial(finish_kernel, S, H, P),
        out_shape=(
            jax.ShapeDtypeStruct((T, D), BF16),
            jax.ShapeDtypeStruct((T, C), BF16),
        ),
        in_specs=[vmem, vmem, hbm, vmem, vmem, vmem, smem, vmem, vmem, vmem],
        out_specs=(vmem, vmem),
        scratch_shapes=[
            pltpu.VMEM((G, T, W), BF16),
            pltpu.VMEM((T, D), F32),
            pltpu.VMEM((taps, T, T + 2 * face), BF16),
            pltpu.VMEM((T + 2 * face, C), BF16),
            pltpu.VMEM((2, face, C), BF16),
            dma, dma((G,)), dma((G,)), dma((2,)), dma((2,)),
        ],
        compiler_params=pltpu.CompilerParams(
            collective_id=1, has_side_effects=True, vmem_limit_bytes=grant
        ),
    )(
        tokens, attn_gate.reshape(1, D), o, w_out, w_dec, conv_weight.reshape(taps, C, C),
        active_blocks, to_next.reshape(1, face), to_prev.reshape(1, face), conv_table,
    )


def solution(mesh):
    rows = P(("seq", "head"), None)
    return jax.shard_map(
        body,
        mesh=mesh,
        in_specs=(
            rows, P(), P(), P(), P(), P(), P(), P(), P(), P(),
            P("seq", None), P(), P(("seq", "head")), P(("seq", "head")), rows,
        ),
        out_specs=(rows, rows),
        check_vma=False,
    )
```

```python
import functools
import math

import jax
import jax.numpy as jnp
from jax import lax
from jax.experimental import pallas as pl
from jax.experimental.pallas import tpu as pltpu
from jax.sharding import PartitionSpec as P

HD = 64
BLK = 64
NB = 8
STEP = 4
UNROLL = 3
KB = 8
EPSILON = 1e-06
MASKED = -1000000000.0
MESH = pl.DeviceIdType.MESH
BF16 = jnp.bfloat16
F32 = jnp.float32


class Group:
    def __init__(self, P, H):
        self.s, self.h = lax.axis_index("seq"), lax.axis_index("head")
        self.P, self.H, self.G, self.half = P, H, P * H, H // 2
        self.chips = self.G // 2
        self.first = self.s - self.s % P
        self.me = (self.s % P) * H + self.h
        self.chip, self.core = self.me // 2, self.me % 2
        self.others = [(0, 1)] + [(i, k) for i in range(1, self.chips) for k in range(2)]

    def chip_at(self, i):
        return (self.chip + i) % self.chips

    def core_at(self, k):
        return (self.core + k) % 2

    def member(self, i, k):
        return self.chip_at(i) * 2 + self.core_at(k)

    def place(self, i, k):
        member = self.member(i, k)
        return (self.first + member // self.H, member % self.H)


def ranges_per_group(S, H, D):
    return 2 if S % 2 == 0 and D // (2 * H) % 128 == 0 else 1


def project_kernel(
    S, H, P,
    tokens, mod_shift, mod_scale, w_qkv, q_gain, k_gain, lists,
    q, kv, all_lists,
    normed, kv_send, q_send, own_sem, list_ssem, list_rsem,
    kv_ssem, kv_rsem, f_ssem, q_ssem, q_rsem,
):
    T, D = tokens.shape
    g = Group(P, H)
    s, h, G, half = g.s, g.h, g.G, g.half
    W = D // G
    WIDE = 2 * W
    has_next, has_prev = g.first + P < S, g.first > 0

    barrier = pltpu.get_barrier_semaphore()
    for i, k in g.others:
        pl.semaphore_signal(barrier, inc=1, device_id=g.place(i, k), device_id_type=MESH)
    for cond, where in ((has_next, (s + P, h)), (has_prev, (s - P, h))):
        @pl.when(cond)
        def _():
            pl.semaphore_signal(barrier, inc=1, device_id=where, device_id_type=MESH)

    RT = 64

    def norm_rows(r, _):
        rows = pl.ds(pl.multiple_of(r * RT, RT), RT)
        x = tokens[rows, :].astype(F32)
        centred = x - jnp.mean(x, axis=-1, keepdims=True)
        spread = jnp.mean(centred * centred, axis=-1, keepdims=True)
        y = centred * lax.rsqrt(spread + EPSILON) * (1.0 + mod_scale[...]) + mod_shift[...]
        normed[rows, :] = y.astype(BF16)
        return 0

    lax.fori_loop(0, T // RT, norm_rows, 0)

    pl.semaphore_wait(
        barrier, G - 1 + jnp.where(has_next, jnp.int32(1), jnp.int32(0)) + jnp.where(has_prev, jnp.int32(1), jnp.int32(0))
    )

    same = (
        lax.broadcasted_iota(jnp.int32, (WIDE, WIDE), 0) // HD
        == lax.broadcasted_iota(jnp.int32, (WIDE, WIDE), 1) // HD
    )
    averaging = jnp.where(same, F32(1.0 / HD), F32(0.0)).astype(BF16)

    def head_norm(x, gain):
        square = x * x
        high = square.astype(BF16)
        low = (square - high.astype(F32)).astype(BF16)
        mean = jnp.dot(high, averaging, preferred_element_type=F32) + jnp.dot(
            low, averaging, preferred_element_type=F32
        )
        return (x * lax.rsqrt(mean + EPSILON) * gain).astype(BF16)

    PT = min(256, T)

    def columns(part, i):
        return pl.ds(pl.multiple_of(part * D + g.chip_at(i) * WIDE, WIDE), WIDE)

    def make_kv(i):
        def step(r, _):
            rows = pl.ds(pl.multiple_of(r * PT, PT), PT)
            x = normed[rows, :]
            key = jnp.dot(x, w_qkv[:, columns(1, i)], preferred_element_type=F32)
            key = head_norm(key, k_gain[:, columns(0, i)])
            val = jnp.dot(x, w_qkv[:, columns(2, i)], preferred_element_type=F32).astype(BF16)
            for core in range(2):
                kv_send[2 * i + core, rows, 0:W] = key[:, core * W : (core + 1) * W]
                kv_send[2 * i + core, rows, W : 2 * W] = val[:, core * W : (core + 1) * W]
            return 0

        lax.fori_loop(0, T // PT, step, 0)

    def make_q(i):
        def step(r, _):
            rows = pl.ds(pl.multiple_of(r * PT, PT), PT)
            x = jnp.dot(normed[rows, :], w_qkv[:, columns(0, i)], preferred_element_type=F32)
            x = head_norm(x, q_gain[:, columns(0, i)])
            for core in range(2):
                q_send[2 * i + core, rows, :] = x[:, core * W : (core + 1) * W]
            return 0

        lax.fori_loop(0, T // PT, step, 0)

    def kv_copy(i, k):
        return pltpu.make_async_remote_copy(
            src_ref=kv_send.at[2 * i + g.core_at(k)],
            dst_ref=kv.at[half + g.me],
            send_sem=kv_ssem.at[2 * i + k],
            recv_sem=kv_rsem.at[half + g.me],
            device_id=g.place(i, k),
            device_id_type=MESH,
        )

    def q_copy(i, k):
        return pltpu.make_async_remote_copy(
            src_ref=q_send.at[2 * i + g.core_at(k)],
            dst_ref=q.at[g.me],
            send_sem=q_ssem.at[2 * i + k],
            recv_sem=q_rsem.at[g.me],
            device_id=g.place(i, k),
            device_id_type=MESH,
        )

    def list_copy(n):
        return pltpu.make_async_remote_copy(
            src_ref=lists,
            dst_ref=all_lists.at[s % P],
            send_sem=list_ssem.at[n],
            recv_sem=list_rsem.at[s % P],
            device_id=(g.first + (s + n) % P, h),
            device_id_type=MESH,
        )

    def forward_copy(i, k, slot, target):
        own = (i, k) == (0, 0)
        return pltpu.make_async_remote_copy(
            src_ref=kv_send.at[g.core] if own else kv.at[half + g.member(i, k)],
            dst_ref=kv.at[slot],
            send_sem=f_ssem.at[2 * i + k],
            recv_sem=kv_rsem.at[slot],
            device_id=(target, h),
            device_id_type=MESH,
        )

    def each_forward(i, k, act):
        owner = g.member(i, k)

        @pl.when(jnp.logical_and(owner >= G - half, has_next))
        def _():
            act(forward_copy(i, k, owner - (G - half), s + P))

        @pl.when(jnp.logical_and(owner < half, has_prev))
        def _():
            act(forward_copy(i, k, half + G + owner, s - P))

    def arrival(ref, slot, sem):
        pltpu.make_async_copy(ref.at[slot], ref.at[slot], sem.at[slot]).wait()

    own_kv = pltpu.make_async_copy(kv_send.at[g.core], kv.at[half + g.me], own_sem.at[0])
    own_q = pltpu.make_async_copy(q_send.at[g.core], q.at[g.me], own_sem.at[1])
    own_list = pltpu.make_async_copy(lists, all_lists.at[s % P], own_sem.at[2])
    own_list.start()
    for n in range(1, P):
        list_copy(n).start()
    for i in list(range(1, g.chips)) + [0]:
        make_kv(i)
        for k in range(2) if i else (1,):
            kv_copy(i, k).start()
    each_forward(0, 0, lambda c: c.start())
    own_kv.start()
    for i in list(range(1, g.chips)) + [0]:
        make_q(i)
        for k in range(2) if i else (1,):
            q_copy(i, k).start()
    own_q.start()
    for i, k in [(0, 1)] + g.others[:0:-1]:
        arrival(kv, half + g.member(i, k), kv_rsem)
        each_forward(i, k, lambda c: c.start())
    for i, k in g.others:
        arrival(q, g.member(i, k), q_rsem)
    for n in range(1, P):
        arrival(all_lists, (s + n) % P, list_rsem)
    for j in range(half):
        @pl.when(has_prev)
        def _():
            arrival(kv, j, kv_rsem)

        @pl.when(has_next)
        def _():
            arrival(kv, half + G + j, kv_rsem)

    own_kv.wait()
    own_q.wait()
    own_list.wait()
    for n in range(1, P):
        list_copy(n).wait_send()
    for i, k in g.others:
        kv_copy(i, k).wait_send()
        q_copy(i, k).wait_send()
    for i, k in [(0, 0)] + g.others:
        each_forward(i, k, lambda c: c.wait_send())


def attend_kernel(H, P, lists, active, q, kv, o):
    G, T, W = q.shape
    heads = W // HD
    group = (lax.axis_index("seq") // P) * G
    o[...] = jnp.zeros_like(o)
    rows_of = lax.broadcasted_iota(jnp.int32, (heads * BLK, W), 0) // BLK
    lanes_of = lax.broadcasted_iota(jnp.int32, (heads * BLK, W), 1) // HD
    diagonal = jnp.where(rows_of == lanes_of, F32(1.0 / math.sqrt(HD)), F32(0.0)).astype(BF16)
    block_of = lax.broadcasted_iota(jnp.int32, (1, KB * BLK), 1) // BLK
    lane_head = lax.broadcasted_iota(jnp.int32, (BLK, W), 1) // HD
    base = (group - H // 2) * NB

    def attend(owner, blocks):
        queries, keys, values, penalties = [], [], [], []
        for b in blocks:
            rows = pl.ds(pl.multiple_of(b * BLK, BLK), BLK)
            queries.append(jnp.concatenate([q[owner, rows, :]] * heads, axis=0) * diagonal)
            picked, penalty = [], jnp.zeros((1, KB * BLK), F32)
            for n in range(KB):
                block = lists[owner // H, n, (owner % H) * NB + b]
                live = lax.rem(block, NB) < active[block // NB]
                penalty = jnp.where(
                    block_of == n, jnp.where(live, F32(0.0), F32(MASKED)), penalty
                )
                picked.append(block - base)
            keys.append(jnp.concatenate([kv[n, :, 0:W] for n in picked], axis=0))
            values.append(jnp.concatenate([kv[n, :, W : 2 * W] for n in picked], axis=0))
            penalties.append(penalty)
        scores = [
            lax.dot_general(x, y, (((1,), (1,)), ((), ())), preferred_element_type=F32) + z
            for x, y, z in zip(queries, keys, penalties)
        ]
        raised = [jnp.exp(x - jnp.max(x, axis=-1, keepdims=True)) for x in scores]
        weights = [
            (x * (1.0 / jnp.sum(x, axis=-1, keepdims=True))).astype(BF16) for x in raised
        ]
        mixed = [jnp.dot(x, y, preferred_element_type=F32) for x, y in zip(weights, values)]
        for b, x in zip(blocks, mixed):
            result = x[0:BLK, :]
            for n in range(1, heads):
                result = jnp.where(lane_head == n, x[n * BLK : (n + 1) * BLK, :], result)
            o[owner, pl.ds(pl.multiple_of(b * BLK, BLK), BLK), :] = result.astype(BF16)

    def each_owner(owner, _):
        def step(b, _):
            attend(owner, [STEP * b + n for n in range(STEP)])
            return 0

        return lax.fori_loop(0, (active[group + owner] + STEP - 1) // STEP, step, 0)

    lax.fori_loop(0, G, each_owner, 0)


def finish_kernel(
    S, H, P,
    tokens, attn_gate, o, w_out, w_dec, conv_w, active, to_next, to_prev, table,
    block_out, decoded,
    att, acc, onehot, buf, face, own_sem, o_ssem, o_rsem, face_ssem, face_rsem,
):
    T, D = tokens.shape
    C = w_dec.shape[1]
    TAPS = table.shape[1]
    FACE = to_next.shape[1]
    RT = 64
    g = Group(P, H)
    s, h, G = g.s, g.h, g.G
    W = D // G
    has_next, has_prev = s < S - 1, s > 0
    wrap_next = jnp.logical_and(g.me == G - 1, has_next)
    wrap_prev = jnp.logical_and(g.me == 0, has_prev)

    barrier = pltpu.get_barrier_semaphore()
    for i, k in g.others:
        pl.semaphore_signal(barrier, inc=1, device_id=g.place(i, k), device_id_type=MESH)
    for cond, where in ((wrap_next, (s + 1, 0)), (wrap_prev, (s - 1, H - 1))):
        @pl.when(cond)
        def _():
            pl.semaphore_signal(barrier, inc=1, device_id=where, device_id_type=MESH)
    pl.semaphore_wait(
        barrier, G - 1 + jnp.where(wrap_next, jnp.int32(1), jnp.int32(0)) + jnp.where(wrap_prev, jnp.int32(1), jnp.int32(0))
    )

    def o_copy(i, k):
        return pltpu.make_async_remote_copy(
            src_ref=o.at[g.member(i, k)],
            dst_ref=att.at[g.me],
            send_sem=o_ssem.at[2 * i + k],
            recv_sem=o_rsem.at[g.me],
            device_id=g.place(i, k),
            device_id_type=MESH,
        )

    own_o = pltpu.make_async_copy(o.at[g.me], att.at[g.me], own_sem)
    for i, k in g.others[::-1]:
        o_copy(i, k).start()
    own_o.start()

    spots = lax.broadcasted_iota(jnp.int32, (T, T + 2 * FACE), 1).astype(F32)
    tap_lane = lax.broadcasted_iota(jnp.int32, (T, TAPS), 1)

    def build(t, _):
        for n in range(UNROLL):
            tap = t * UNROLL + n
            want = jnp.sum(
                jnp.where(tap_lane == tap, table[...].astype(F32), 0.0), axis=1, keepdims=True
            )
            onehot[tap] = jnp.where(spots == want, F32(1.0), F32(0.0)).astype(BF16)
        return 0

    lax.fori_loop(0, TAPS // UNROLL, build, 0)

    own_o.wait()
    for i, k in g.others:
        owner = g.member(i, k)
        pltpu.make_async_copy(att.at[owner], att.at[owner], o_rsem.at[owner]).wait()
    attended = jnp.concatenate([att[n] for n in range(G)], axis=1)
    acc[...] = jnp.dot(attended, w_out[...], preferred_element_type=F32)

    own_live = active[s * H + h] * BLK

    def finish(r, _):
        rows = pl.ds(pl.multiple_of(r * RT, RT), RT)
        live = lax.broadcasted_iota(jnp.int32, (RT, 1), 0) + r * RT < own_live
        residual = tokens[rows, :].astype(F32) + attn_gate[...] * acc[rows, :]
        block_out[rows, :] = jnp.where(live, residual, 0.0).astype(BF16)
        return 0

    lax.fori_loop(0, T // RT, finish, 0)
    features = jnp.dot(block_out[...], w_dec[...], preferred_element_type=F32).astype(BF16)
    buf[0:T, :] = features

    slots = lax.broadcasted_iota(jnp.int32, (T, FACE), 0)
    for n, ref in enumerate((to_next, to_prev)):
        chosen = jnp.where(slots == ref[...], F32(1.0), F32(0.0)).astype(BF16)
        face[n] = lax.dot_general(
            chosen, features, (((0,), (0,)), ((), ())), preferred_element_type=F32
        ).astype(BF16)

    def face_copy(n, target):
        return pltpu.make_async_remote_copy(
            src_ref=face.at[n],
            dst_ref=buf.at[pl.ds(T + n * FACE, FACE), :],
            send_sem=face_ssem.at[n],
            recv_sem=face_rsem.at[n],
            device_id=target,
            device_id_type=MESH,
        )

    any_next = jnp.logical_or(has_next, h < H - 1)
    any_prev = jnp.logical_or(has_prev, h > 0)
    device = s * H + h

    @pl.when(any_next)
    def _():
        face_copy(0, ((device + 1) // H, (device + 1) % H)).start()

    @pl.when(any_prev)
    def _():
        face_copy(1, ((device - 1) // H, (device - 1) % H)).start()

    def face_arrival(n):
        rows = buf.at[pl.ds(T + n * FACE, FACE), :]
        pltpu.make_async_copy(rows, rows, face_rsem.at[n]).wait()

    for n, cond in ((0, any_prev), (1, any_next)):
        @pl.when(cond)
        def _():
            face_arrival(n)

        @pl.when(jnp.logical_not(cond))
        def _():
            buf[T + n * FACE : T + (n + 1) * FACE, :] = jnp.zeros((FACE, C), BF16)

    acc[:, 0:C] = buf[0:T, :].astype(F32)

    def taps(t, _):
        rows = jnp.concatenate(
            [
                jnp.dot(onehot[t * UNROLL + n], buf[...], preferred_element_type=F32).astype(BF16)
                for n in range(UNROLL)
            ],
            axis=1,
        )
        weights = conv_w[pl.ds(pl.multiple_of(t * UNROLL * C, C), UNROLL * C), :]
        acc[:, 0:C] += jnp.dot(rows, weights, preferred_element_type=F32)
        return 0

    lax.fori_loop(0, TAPS // UNROLL, taps, 0)
    total = acc[:, 0:C]
    live = lax.broadcasted_iota(jnp.int32, (T, 1), 0) < own_live
    decoded[...] = jnp.where(live, total, 0.0).astype(BF16)

    for i, k in g.others:
        o_copy(i, k).wait_send()

    @pl.when(any_next)
    def _():
        face_copy(0, ((device + 1) // H, (device + 1) % H)).wait_send()

    @pl.when(any_prev)
    def _():
        face_copy(1, ((device - 1) // H, (device - 1) % H)).wait_send()


def body(
    tokens, mod_shift, mod_scale, attn_gate, w_qkv, query_gain, key_gain, w_out, w_dec,
    conv_weight, block_lists, active_blocks, to_next, to_prev, conv_table,
):
    S, H = lax.axis_size("seq"), lax.axis_size("head")
    T, D = tokens.shape
    P = ranges_per_group(S, H, D)
    G = P * H
    W = D // G
    C = w_dec.shape[1]
    taps = conv_table.shape[1]
    face = to_next.shape[0]
    vmem = pl.BlockSpec(memory_space=pltpu.VMEM)
    smem = pl.BlockSpec(memory_space=pltpu.SMEM)
    hbm = pl.BlockSpec(memory_space=pl.ANY)
    dma = pltpu.SemaphoreType.DMA
    grant = 60 * 1024 * 1024
    q, kv, lists = pl.pallas_call(
        functools.partial(project_kernel, S, H, P),
        out_shape=(
            jax.ShapeDtypeStruct((G, T, W), BF16),
            jax.ShapeDtypeStruct((G + H, T, 2 * W), BF16),
            jax.ShapeDtypeStruct((P, KB, block_lists.shape[0]), jnp.int32),
        ),
        in_specs=[vmem] * 6 + [hbm],
        out_specs=(hbm, hbm, hbm),
        scratch_shapes=[
            pltpu.VMEM((T, D), BF16),
            pltpu.VMEM((G, T, 2 * W), BF16),
            pltpu.VMEM((G, T, W), BF16),
            dma((3,)), dma((P,)), dma((P,)),
            dma((G,)), dma((G + H,)), dma((G,)),
            dma((G,)), dma((G,)),
        ],
        compiler_params=pltpu.CompilerParams(
            collective_id=0, has_side_effects=True, vmem_limit_bytes=grant
        ),
    )(
        tokens, mod_shift.reshape(1, D), mod_scale.reshape(1, D), w_qkv,
        query_gain.reshape(1, D), key_gain.reshape(1, D), block_lists.T,
    )
    o = pl.pallas_call(
        functools.partial(attend_kernel, H, P),
        out_shape=jax.ShapeDtypeStruct((G, T, W), BF16),
        in_specs=[smem, smem, vmem, vmem],
        out_specs=vmem,
        compiler_params=pltpu.CompilerParams(vmem_limit_bytes=grant),
    )(lists, active_blocks, q, kv.reshape((G + H) * NB, BLK, 2 * W))
    return pl.pallas_call(
        functools.partial(finish_kernel, S, H, P),
        out_shape=(
            jax.ShapeDtypeStruct((T, D), BF16),
            jax.ShapeDtypeStruct((T, C), BF16),
        ),
        in_specs=[vmem, vmem, hbm, vmem, vmem, vmem, smem, vmem, vmem, vmem],
        out_specs=(vmem, vmem),
        scratch_shapes=[
            pltpu.VMEM((G, T, W), BF16),
            pltpu.VMEM((T, D), F32),
            pltpu.VMEM((taps, T, T + 2 * face), BF16),
            pltpu.VMEM((T + 2 * face, C), BF16),
            pltpu.VMEM((2, face, C), BF16),
            dma, dma((G,)), dma((G,)), dma((2,)), dma((2,)),
        ],
        compiler_params=pltpu.CompilerParams(
            collective_id=1, has_side_effects=True, vmem_limit_bytes=grant
        ),
    )(
        tokens, attn_gate.reshape(1, D), o, w_out, w_dec, conv_weight,
        active_blocks, to_next.reshape(1, face), to_prev.reshape(1, face), conv_table,
    )


def solution(mesh):
    rows = P(("seq", "head"), None)
    return jax.shard_map(
        body,
        mesh=mesh,
        in_specs=(
            rows, P(), P(), P(), P(), P(), P(), P(), P(), P(),
            P("seq", None), P(), P(("seq", "head")), P(("seq", "head")), rows,
        ),
        out_specs=(rows, rows),
        check_vma=False,
    )
```
